256 devices in a mesh: tm: 64 (over y, z_lo, x, core), floor: 4 (over z_hi).
Axes of the slice: x: 4, y: 4, z: 8 (z_hi: 4, z_lo: 2; z = z_hi * 2 + z_lo), core: 2. Of those that a mesh axis runs over, the one named last changes fastest.
Arguments:
- samples: bfloat16 [64, 16, 32768], P('tm', None, 'floor'), may hold values from -6 to 6
- operator: bfloat16 [64, 512, 32768], P('tm', None, 'floor'), may hold values from -0.00390625 to 0.00390625
Outputs:
- sensor_data: bfloat16 [64, 16, 512], P('tm', None, 'floor')
The draws below stay inside these ranges and needn't reach their ends.
All inputs are finite; a program needn't handle non-finite values.
Results may differ from the reference program's by a relative error of at most 0.0013.
Values may be sent and summed in bfloat16 or wider, within the bound.
No kernel may reach another device: no remote copies, remote signals or barrier semaphores. Data moves between devices by JAX's collectives and lax.ppermute only.
A program may use at most 64 MiB of HBM per device.

```python
import jax
import jax.numpy as jnp
from jax import lax

S = 512
P_SIZE = 32768
K = 16
NT = 64


def level_of(key, shape, cuts, low, high):
    def one(dim, parts):
        heights = jax.random.uniform(jax.random.fold_in(jax.random.fold_in(key, 6), dim), (parts,), jnp.float32, low / len(cuts), high / len(cuts))
        return jnp.repeat(jnp.exp(heights), shape[dim] // parts).reshape((-1,) + (1,) * (len(shape) - dim - 1))

    factor_of = one(*cuts[0])
    for cut in cuts[1:]:
        factor_of = factor_of * one(*cut)
    return factor_of


def noise(rng, dims, width, bound, pieces=(), kind=jnp.bfloat16):
    result = jax.random.normal(rng, dims, jnp.float32) * width
    if len(pieces) > 0:
        result = level_of(rng, dims, pieces, -0.22, 0.18) * result
    return jnp.clip(result, min=-bound, max=bound).astype(kind)


def setup_inputs(seed: int = 0) -> dict:
    splits = jax.random.split(jax.random.key(seed), 3)
    return {
        "samples": noise(splits[0], (NT, K, P_SIZE), 1.0, 6.0, ((0, 64), (2, 4))),
        "operator": noise(splits[1], (NT, S, P_SIZE), (P_SIZE * NT) ** -0.5, 0.00390625, ((0, 64), (2, 4))),
    }


def reference(samples, operator):
    blocks = samples.astype(jnp.float32)

    def add_lag(total, lag):
        kernel = lax.dynamic_index_in_dim(operator, lag, 0, keepdims=False).astype(jnp.float32)
        images = jnp.einsum('tki,si->tks', blocks, kernel)
        padded = jnp.pad(images, ((NT, 0), (0, 0), (0, 0)))
        shifted = lax.dynamic_slice_in_dim(padded, (NT - lag).astype(jnp.int32), NT, 0)
        return total + shifted, None

    start = jnp.zeros((NT, K, S), jnp.float32)
    total, _ = lax.scan(add_lag, start, jnp.arange(NT, dtype=jnp.int32))
    return total.astype(jnp.bfloat16)
```

```python
import jax
import jax.numpy as jnp
from jax import lax
from jax.sharding import PartitionSpec as P


def local(samples, operator):
    lag = lax.axis_index("tm")
    blocks = lax.axis_size("tm")
    kernel = operator[0]
    images = jnp.einsum(
        "cki,si->cks",
        lax.all_gather(samples, "tm", axis=0, tiled=True),
        kernel,
        preferred_element_type=jnp.float32,
    )
    padded = jnp.pad(images, ((blocks, 0), (0, 0), (0, 0)))
    shifted = lax.dynamic_slice_in_dim(padded, blocks - lag, blocks, 0)
    mine = lax.all_to_all(shifted, "tm", 0, 0, tiled=True).sum(0)
    parts = mine.reshape(mine.shape[0], lax.axis_size("floor"), -1).swapaxes(0, 1)
    records = lax.all_to_all(parts, "floor", 0, 0, tiled=True).sum(0)
    return records[None].astype(jnp.bfloat16)


def solution(mesh):
    placed = (P("tm", None, "floor"), P("tm", None, "floor"))
    return jax.shard_map(
        local, mesh=mesh, in_specs=placed, out_specs=P("tm", None, "floor"), check_vma=False
    )
```

```python
import functools

import jax
import jax.numpy as jnp
from jax import lax
from jax.experimental import pallas as pl
from jax.experimental.pallas import tpu as pltpu
from jax.sharding import PartitionSpec as P

Y, Z, X, CORES = 4, 2, 4, 2
CHIPS = Y * Z * X

XP, XM, YP, YM, ZZ = (1, 0, 0), (3, 0, 0), (0, 1, 0), (0, 3, 0), (0, 0, 1)
LINKS = (XP, XM, YP, YM, ZZ)
SLOTS = (
    ((1, 0, 0), (3, 0, 0), (0, 1, 0), (0, 3, 0), (0, 0, 1)),
    ((1, 1, 0), (3, 3, 0), (0, 2, 0), (1, 3, 0), (3, 0, 1)),
    ((2, 0, 0), (3, 1, 0), (0, 1, 1), (0, 3, 1), (1, 0, 1)),
    ((2, 1, 0), (2, 3, 0), (3, 1, 1), (1, 2, 0), (0, 2, 1)),
    ((1, 1, 1), (3, 3, 1), (3, 2, 0), (1, 3, 1), (2, 0, 1)),
    ((1, 2, 1), (2, 1, 1), (3, 2, 1), (2, 2, 0), (2, 3, 1)),
)
OWN, LAST = (0, 0, 0), (2, 2, 1)
EARLY = (OWN,) + SLOTS[0] + SLOTS[1] + SLOTS[2]
LATE = SLOTS[3] + SLOTS[4] + SLOTS[5] + (LAST,)


def number(y, z, x, core):
    return ((y * Z + z) * X + x) * CORES + core


def moved(d, link):
    return ((d[0] - link[0]) % X, (d[1] - link[1]) % Y, (d[2] - link[2]) % Z)


def pairs(link):
    return [
        (number(y, z, x, c), number((y + link[1]) % Y, (z + link[2]) % Z, (x + link[0]) % X, c))
        for y in range(Y)
        for z in range(Z)
        for x in range(X)
        for c in range(CORES)
    ]


OTHER_CORE = [(2 * i + c, 2 * i + 1 - c) for i in range(CHIPS) for c in range(CORES)]
SAME_CORE = [[2 * i + c for i in range(CHIPS)] for c in range(CORES)]


def gather(block):
    held = {OWN: block}
    for slot in SLOTS:
        for link, d in zip(LINKS, slot):
            held[d] = lax.ppermute(held[moved(d, link)], "tm", pairs(link))
    lanes = block.shape[-1] // 128
    cuts = [128 * (lanes * n // len(LINKS)) for n in range(len(LINKS) + 1)]
    held[LAST] = jnp.concatenate(
        [
            lax.ppermute(held[moved(LAST, link)][:, a:b], "tm", pairs(link))
            for link, a, b in zip(LINKS, cuts, cuts[1:])
        ],
        axis=1,
    )
    return held


def source(me, d):
    chip = me // CORES
    x, z, y = chip % X, (chip // X) % Z, chip // (X * Z)
    return (((y - d[1] + Y) % Y) * Z + (z - d[2] + Z) % Z) * X + (x - d[0] + X) % X


def product(blocks, weights, depth):
    total = None
    for k in range(0, weights.shape[1], depth):
        rows = jnp.concatenate([b[:, k : k + depth] for b in blocks], axis=0)
        term = lax.dot_general(
            rows,
            weights[:, k : k + depth],
            (((1,), (1,)), ((), ())),
            preferred_element_type=jnp.float32,
        )
        total = term if total is None else total + term
    return total


def early_kernel(count, steps, depth, *refs):
    blocks, (own, other, out) = refs[:count], refs[count:]
    n = pl.program_id(0)

    @pl.when(n < steps)
    def _():
        out[0] = product(blocks, own, depth)

    @pl.when(n >= steps)
    def _():
        out[0] = product(blocks, other, depth)


def late_kernel(count, steps, depth, *refs):
    me_ref, refs = refs[0], refs[1:]
    blocks, (own, other, early, keep, send) = refs[:count], refs[count:]
    n = pl.program_id(0)
    me = me_ref[0]
    core, chip = me % CORES, me // CORES
    k = blocks[0].shape[0]
    width = own.shape[0]

    def place(which, rows, offsets, columns):
        first = chip + (core if which == 0 else 0)
        keeps = core == which
        for b, d in enumerate(offsets):
            to = source(me, d) + first

            @pl.when(jnp.logical_and(to < CHIPS, keeps))
            def _():
                keep[to, :, columns] = rows[b * k : (b + 1) * k]

            @pl.when(jnp.logical_and(to < CHIPS, jnp.logical_not(keeps)))
            def _():
                send[to, :, columns] = rows[b * k : (b + 1) * k]

    @pl.when(n == 0)
    def _():
        keep[...] = jnp.zeros_like(keep)
        send[...] = jnp.zeros_like(send)
        for which in range(2):
            place(which, early.at[which], EARLY, slice(None))

    for which, weights in enumerate((own, other)):
        for step in range(steps):

            @pl.when(n == which * steps + step)
            def _():
                place(
                    which,
                    product(blocks, weights, depth),
                    LATE,
                    slice(step * width, (step + 1) * width),
                )


def specs(blocks, own, tile):
    k, p = blocks[0].shape
    steps = own.shape[0] // tile
    whole = pl.BlockSpec((k, p), lambda n, *_: (0, 0))
    first = pl.BlockSpec((tile, p), lambda n, *_: (jnp.minimum(n, steps - 1), 0))
    second = pl.BlockSpec((tile, p), lambda n, *_: (jnp.maximum(n - steps, 0), 0))
    return steps, [whole] * len(blocks) + [first, second]


def cost(blocks, own):
    k, p = blocks[0].shape
    rows, s = k * len(blocks), own.shape[0]
    return pl.CostEstimate(
        flops=4 * rows * p * s, bytes_accessed=2 * p * (rows + 2 * s) + 8 * rows * s, transcendentals=0
    )


TILE, DEPTH, VMEM = 256, 2048, 48 << 20


def multiply_early(blocks, own, other):
    rows, s = blocks[0].shape[0] * len(blocks), own.shape[0]
    steps, in_specs = specs(blocks, own, TILE)
    return pl.pallas_call(
        functools.partial(early_kernel, len(blocks), steps, DEPTH),
        out_shape=jax.ShapeDtypeStruct((2, rows, s), jnp.float32),
        grid=(2 * steps,),
        in_specs=in_specs,
        out_specs=pl.BlockSpec((1, rows, TILE), lambda n: (n // steps, 0, n % steps)),
        compiler_params=pltpu.CompilerParams(vmem_limit_bytes=VMEM),
        cost_estimate=cost(blocks, own),
        name="early",
    )(*blocks, own, other)


def multiply_late(me, blocks, own, other, early):
    k, s = blocks[0].shape[0], own.shape[0]
    steps, in_specs = specs(blocks, own, TILE)
    out = jax.ShapeDtypeStruct((CHIPS, k, s), jnp.float32)
    out_spec = pl.BlockSpec((CHIPS, k, s), lambda n, *_: (0, 0, 0))
    return pl.pallas_call(
        functools.partial(late_kernel, len(blocks), steps, DEPTH),
        out_shape=[out, out],
        grid_spec=pltpu.PrefetchScalarGridSpec(
            num_scalar_prefetch=1,
            grid=(2 * steps,),
            in_specs=in_specs + [pl.BlockSpec(early.shape, lambda n, *_: (0, 0, 0))],
            out_specs=[out_spec, out_spec],
        ),
        compiler_params=pltpu.CompilerParams(vmem_limit_bytes=VMEM),
        cost_estimate=cost(blocks, own),
        name="late",
    )(me, *blocks, own, other, early)


def local(samples, operator):
    me = lax.axis_index("tm")
    own = operator[0]
    held = gather(samples[0])
    other = lax.ppermute(own, "tm", OTHER_CORE)
    early = multiply_early([held[d] for d in EARLY], own, other)
    keep, send = multiply_late(me.reshape(1), [held[d] for d in LATE], own, other, early)
    both = keep + lax.ppermute(send, "tm", OTHER_CORE)
    mine = lax.all_to_all(both, "tm", 0, 0, tiled=True, axis_index_groups=SAME_CORE).sum(0)
    parts = mine.reshape(mine.shape[0], lax.axis_size("floor"), -1).swapaxes(0, 1)
    records = lax.all_to_all(parts, "floor", 0, 0, tiled=True).sum(0)
    return records[None].astype(jnp.bfloat16)


def solution(mesh):
    placed = (P("tm", None, "floor"), P("tm", None, "floor"))
    return jax.shard_map(
        local, mesh=mesh, in_specs=placed, out_specs=P("tm", None, "floor"), check_vma=False
    )
```

```python
import functools

import jax
import jax.numpy as jnp
from jax import lax
from jax.experimental import pallas as pl
from jax.experimental.pallas import tpu as pltpu
from jax.sharding import PartitionSpec as P

Y, Z, X, CORES = 4, 2, 4, 2
CHIPS = Y * Z * X

XP, XM, YP, YM, ZZ = (1, 0, 0), (3, 0, 0), (0, 1, 0), (0, 3, 0), (0, 0, 1)
LINKS = (XP, XM, YP, YM, ZZ)
OWN, LAST = (0, 0, 0), (2, 2, 1)
DETOURS = ((3, 1, 0), (3, 3, 0))
PHASES = (
    ((XM, ((3, 0, 0),)), (YP, ((0, 1, 0),)), (ZZ, ((0, 0, 1),)), (XP, ((1, 0, 0),)), (YM, ((0, 3, 0),))),
    (
        (YP, ((0, 2, 0), (3, 1, 0))),
        (XM, ((2, 0, 0), (3, 0, 1))),
        (XP, ((1, 0, 1), (1, 1, 0))),
        (YM, ((1, 3, 0), (3, 3, 0))),
    ),
    (
        (XM, ((3, 2, 0), (2, 1, 0))),
        (YM, ((2, 3, 0), (3, 3, 1))),
        (YP, ((1, 1, 1), (3, 1, 1))),
        (ZZ, ((0, 2, 1), (1, 3, 1))),
        (XP, ((2, 0, 1), (1, 2, 0))),
    ),
    (
        (ZZ, ((0, 1, 1), (0, 3, 1))),
        (XP, ((2, 1, 1), (2, 2, 0))),
        (XM, ((2, 3, 1),)),
        (YP, ((1, 2, 1),)),
        (YM, ((3, 2, 1),)),
    ),
)


def number(y, z, x, core):
    return ((y * Z + z) * X + x) * CORES + core


def moved(d, link):
    return ((d[0] - link[0]) % X, (d[1] - link[1]) % Y, (d[2] - link[2]) % Z)


def pairs(link):
    return [
        (number(y, z, x, c), number((y + link[1]) % Y, (z + link[2]) % Z, (x + link[0]) % X, c))
        for y in range(Y)
        for z in range(Z)
        for x in range(X)
        for c in range(CORES)
    ]


OTHER_CORE = [(2 * i + c, 2 * i + 1 - c) for i in range(CHIPS) for c in range(CORES)]
SAME_CORE = [[2 * i + c for i in range(CHIPS)] for c in range(CORES)]


def fetch(held, wanted):
    for names, rows in held:
        if names == wanted:
            return rows
    k = held[0][1].shape[0] // len(held[0][0])
    parts = []
    for name in wanted:
        names, rows = next((n, r) for n, r in held if name in n)
        at = names.index(name) * k
        parts.append(rows if len(names) == 1 else rows[at : at + k])
    return parts[0] if len(parts) == 1 else jnp.concatenate(parts, axis=0)


def after(value, *others):
    return lax.optimization_barrier((value, *others))[0]


def send(held, phase, chain, waits=()):
    rows = [fetch(held, tuple(moved(d, link) for d in names)) for link, names in phase]
    got = []
    for (link, names), r in zip(phase, rows):
        ties = chain.get(link, []) + list(waits)
        if ties:
            r = after(r, *ties)
        chain[link] = [lax.ppermute(r, "tm", pairs(link))]
        got.append((names, chain[link][0]))
    return got


def send_last(held, wait):
    rows = [fetch(held, (moved(LAST, route),)) for route in DETOURS]
    k = rows[0].shape[0] // len(DETOURS)
    return [
        lax.ppermute(after(r[n * k : (n + 1) * k], wait), "tm", pairs(route))
        for n, (route, r) in enumerate(zip(DETOURS, rows))
    ]


def source(me, d):
    chip = me // CORES
    x, z, y = chip % X, (chip // X) % Z, chip // (X * Z)
    return (((y - d[1] + Y) % Y) * Z + (z - d[2] + Z) % Z) * X + (x - d[0] + X) % X


def multiply_kernel(names, count, k, steps, first, *refs):
    me_ref, refs = refs[0], refs[1:]
    bundles, refs = refs[:count], refs[count:]
    weights, refs = refs[:CORES], refs[CORES:]
    keep, out, rows = refs[-3:]
    n = pl.program_id(0)
    me = me_ref[0]
    core, chip = me % CORES, me // CORES
    width = weights[0].shape[0] // steps

    @pl.when(n == 0)
    def _():
        if first:
            keep[...] = jnp.zeros_like(keep)
            out[...] = jnp.zeros_like(out)
        else:
            keep[...] = refs[0][...]
            out[...] = refs[1][...]

    def place(even, odd, shift, columns):
        for b, d in enumerate(names):
            to = source(me, d) + chip
            after = to + shift

            @pl.when(to < CHIPS)
            def _():
                even[to, :, columns] += rows[2 * b * k : (2 * b + 1) * k]

            @pl.when(after < CHIPS)
            def _():
                odd[after, :, columns] += rows[(2 * b + 1) * k : (2 * b + 2) * k]

    for which, tiles in enumerate(weights):
        for step in range(steps):

            @pl.when(n == which * steps + step)
            def _():
                left = jnp.concatenate([b[...] for b in bundles], axis=0)
                rows[...] = lax.dot_general(
                    left,
                    tiles[step * width : (step + 1) * width],
                    (((1,), (1,)), ((), ())),
                    preferred_element_type=jnp.float32,
                )

    for step in range(steps):
        columns = slice(step * width, (step + 1) * width)

        @pl.when(n == step)
        def _():
            place(keep, out, core, columns)

        @pl.when(n == steps + step)
        def _():
            place(out, keep, 1 - core, columns)


TILE, VMEM = 256, 18 << 20


def multiply(me, names, bundles, weights, before, name):
    total, p = sum(r.shape[0] for r in bundles), bundles[0].shape[1]
    s = weights[0].shape[0]
    k, steps = total // (2 * len(names)), s // TILE
    once = pl.Buffered(1)
    kept = pl.BlockSpec((CHIPS, k, s), lambda n, me: (0, 0, 0), pipeline_mode=once)
    whole = [
        pl.BlockSpec(r.shape, lambda n, me: (0, 0), pipeline_mode=once) for r in (*bundles, *weights)
    ]
    out = jax.ShapeDtypeStruct((CHIPS, k, s), jnp.float32)
    return pl.pallas_call(
        functools.partial(multiply_kernel, names, len(bundles), k, steps, not before),
        out_shape=[out, out],
        grid_spec=pltpu.PrefetchScalarGridSpec(
            num_scalar_prefetch=1,
            grid=(2 * steps,),
            in_specs=whole + [kept] * len(before),
            out_specs=[kept, kept],
            scratch_shapes=[pltpu.VMEM((total, TILE), jnp.float32)],
        ),
        compiler_params=pltpu.CompilerParams(vmem_limit_bytes=VMEM),
        cost_estimate=pl.CostEstimate(
            flops=4 * total * p * s, bytes_accessed=2 * p * (total + 2 * s) + 16 * CHIPS * k * s, transcendentals=0
        ),
        name=name,
    )(me, *bundles, *weights, *before)


def across_floors(rows, at):
    width = rows.shape[1] // len(at)

    def parts(*owners):
        return jnp.concatenate(
            [lax.dynamic_slice_in_dim(rows, q * width, width, 1) for q in owners], axis=1
        )

    def swap(value, by):
        return lax.ppermute(value, "floor", [(f, f ^ by) for f in range(len(at))])

    two = parts(at[0], at[3]) + swap(parts(at[1], at[2]), 1)
    return two[:, :width] + swap(two[:, width:], 3)


def local(samples, operator):
    me = lax.axis_index("tm")
    core = me % CORES
    half = samples.shape[2] // CORES
    own = operator[0]

    def columns(rows, which):
        return lax.dynamic_slice_in_dim(rows, which * half, half, 1)

    theirs = lax.ppermute(columns(samples[0], 1 - core), "tm", OTHER_CORE)
    mine = columns(samples[0], core)
    block = jnp.concatenate(
        [jnp.where(core == 0, mine, theirs), jnp.where(core == 0, theirs, mine)], axis=0
    )
    at = me.reshape(1)

    def names(bundles):
        return [d for n, _ in bundles for d in n]

    def rows(bundles):
        return [r for _, r in bundles]

    chain = {}
    held = [((OWN,), block)]
    held = held + send(held, PHASES[0], chain)
    other = columns(after(own, block), 1 - core)
    other = lax.ppermute(after(other, *rows(held)), "tm", OTHER_CORE)
    chain[ZZ] = [other]
    weights = (columns(after(own, *rows(held)), core), other)
    held = held + send(held, PHASES[1], chain)
    got = send(held, PHASES[2], chain, (other,))
    early = multiply(at, names(held), rows(held), weights, (), "early")
    mid_blocks = got
    last = send_last(held + mid_blocks, early[0])
    got = send(held + mid_blocks, PHASES[3], chain, early[:1])
    mid = multiply(at, names(mid_blocks), rows(mid_blocks), weights, early, "mid")
    keep, out = multiply(
        at, names(got) + [LAST], rows(got) + last, weights, mid, "late"
    )

    both = keep + lax.ppermute(out, "tm", OTHER_CORE)
    floor = lax.axis_index("floor")
    floors = [floor ^ n for n in range(lax.axis_size("floor"))]
    sums = lax.all_to_all(both, "tm", 0, 0, tiled=True, axis_index_groups=SAME_CORE).sum(0)
    return across_floors(sums, floors)[None].astype(jnp.bfloat16)


def solution(mesh):
    placed = (P("tm", None, "floor"), P("tm", None, "floor"))
    return jax.shard_map(
        local, mesh=mesh, in_specs=placed, out_specs=P("tm", None, "floor"), check_vma=False
    )
```

```python
import functools

import jax
import jax.numpy as jnp
from jax import lax
from jax.experimental import pallas as pl
from jax.experimental.pallas import tpu as pltpu
from jax.sharding import PartitionSpec as P

Y, Z, X, CORES = 4, 2, 4, 2
CHIPS = Y * Z * X

XP, XM, YP, YM, ZZ = (1, 0, 0), (3, 0, 0), (0, 1, 0), (0, 3, 0), (0, 0, 1)
LINKS = (XP, XM, YP, YM, ZZ)
OWN, LAST = (0, 0, 0), (2, 2, 1)
FINISH = (XM, YM)
PHASES = (
    ((XM, ((3, 0, 0),)), (YP, ((0, 1, 0),)), (ZZ, ((0, 0, 1),)), (XP, ((1, 0, 0),)), (YM, ((0, 3, 0),))),
    (
        (YP, ((0, 2, 0), (3, 1, 0))),
        (XM, ((2, 0, 0), (3, 0, 1))),
        (XP, ((1, 0, 1), (1, 1, 0))),
        (YM, ((1, 3, 0), (3, 3, 0))),
    ),
    (
        (XM, ((3, 2, 0), (2, 1, 0))),
        (YM, ((2, 3, 0), (3, 3, 1))),
        (YP, ((1, 1, 1), (3, 1, 1))),
        (ZZ, ((0, 2, 1), (1, 3, 1))),
        (XP, ((2, 0, 1), (1, 2, 0))),
    ),
    ((ZZ, ((0, 1, 1), (0, 3, 1))), (YM, ((3, 2, 1),)), (XM, ((2, 3, 1),))),
)
SHARED = (2, 2, 0)
SHARING = ((XP, (2, 1, 1)), (YP, (1, 2, 1)))


def number(y, z, x, core):
    return ((y * Z + z) * X + x) * CORES + core


def moved(d, link):
    return ((d[0] - link[0]) % X, (d[1] - link[1]) % Y, (d[2] - link[2]) % Z)


def pairs(link):
    return [
        (number(y, z, x, c), number((y + link[1]) % Y, (z + link[2]) % Z, (x + link[0]) % X, c))
        for y in range(Y)
        for z in range(Z)
        for x in range(X)
        for c in range(CORES)
    ]


OTHER_CORE = [(2 * i + c, 2 * i + 1 - c) for i in range(CHIPS) for c in range(CORES)]
SAME_CORE = [[2 * i + c for i in range(CHIPS)] for c in range(CORES)]


def fetch(held, wanted):
    for names, rows in held:
        if names == wanted:
            return rows
    k = held[0][1].shape[0] // len(held[0][0])
    parts = []
    for name in wanted:
        names, rows = next((n, r) for n, r in held if name in n)
        at = names.index(name) * k
        parts.append(rows if len(names) == 1 else rows[at : at + k])
    return parts[0] if len(parts) == 1 else jnp.concatenate(parts, axis=0)


def after(value, *others):
    return lax.optimization_barrier((value, *others))[0]


def send(held, phase, chain, waits=(), sent=None):
    rows = [fetch(held, tuple(moved(d, link) for d in names)) for link, names in phase]
    got = []
    for (link, names), r in zip(phase, rows):
        ties = chain.get(link, []) + list(waits)
        if ties:
            r = after(r, *ties)
        if sent is not None:
            sent.append(r)
        chain[link] = [lax.ppermute(r, "tm", pairs(link))]
        got.append((names, chain[link][0]))
    return got


def send_last(held, chain, wait):
    rows = [fetch(held, (moved(LAST, link),)) for link in FINISH]
    k = rows[0].shape[0] // len(FINISH)
    return [
        lax.ppermute(after(r[n * k : (n + 1) * k], wait, *chain[link]), "tm", pairs(link))
        for n, (link, r) in enumerate(zip(FINISH, rows))
    ]


def send_shared(held, chain, wait):
    (first, before), (second, behind) = SHARING
    k = held[0][1].shape[0] // len(held[0][0])
    parts = (
        (first, [fetch(held, (moved(before, first),)), fetch(held, (moved(SHARED, first),))[: k // 2]]),
        (second, [fetch(held, (moved(SHARED, second),))[k // 2 :], fetch(held, (moved(behind, second),))]),
    )
    got = []
    for link, rows in parts:
        rows = after(jnp.concatenate(rows, axis=0), wait, *chain[link])
        chain[link] = [lax.ppermute(rows, "tm", pairs(link))]
        got.append(chain[link][0])
    return got


def source(me, d):
    chip = me // CORES
    x, z, y = chip % X, (chip // X) % Z, chip // (X * Z)
    return (((y - d[1] + Y) % Y) * Z + (z - d[2] + Z) % Z) * X + (x - d[0] + X) % X


def multiply_kernel(names, count, k, steps, first, *refs):
    me_ref, refs = refs[0], refs[1:]
    bundles, refs = refs[:count], refs[count:]
    weights, refs = refs[:CORES], refs[CORES:]
    keep, out, rows = refs[-3:]
    n = pl.program_id(0)
    me = me_ref[0]
    core, chip = me % CORES, me // CORES
    width = weights[0].shape[0] // steps

    @pl.when(n == 0)
    def _():
        if first:
            keep[...] = jnp.zeros_like(keep)
            out[...] = jnp.zeros_like(out)
        else:
            keep[...] = refs[0][...]
            out[...] = refs[1][...]

    def place(even, odd, shift, columns):
        for b, d in enumerate(names):
            to = source(me, d) + chip
            after = to + shift

            @pl.when(to < CHIPS)
            def _():
                even[to, :, columns] += rows[2 * b * k : (2 * b + 1) * k]

            @pl.when(after < CHIPS)
            def _():
                odd[after, :, columns] += rows[(2 * b + 1) * k : (2 * b + 2) * k]

    for which, tiles in enumerate(weights):
        for step in range(steps):

            @pl.when(n == which * steps + step)
            def _():
                left = jnp.concatenate([b[...] for b in bundles], axis=0)
                rows[...] = lax.dot_general(
                    left,
                    tiles[step * width : (step + 1) * width],
                    (((1,), (1,)), ((), ())),
                    preferred_element_type=jnp.float32,
                )

    for step in range(steps):
        columns = slice(step * width, (step + 1) * width)

        @pl.when(n == step)
        def _():
            place(keep, out, core, columns)

        @pl.when(n == steps + step)
        def _():
            place(out, keep, 1 - core, columns)


TILE = 256


def multiply(me, names, bundles, weights, before, name):
    total, p = sum(r.shape[0] for r in bundles), bundles[0].shape[1]
    s = weights[0].shape[0]
    k, steps = total // (2 * len(names)), s // TILE
    once = pl.Buffered(1)
    kept = pl.BlockSpec((CHIPS, k, s), lambda n, me: (0, 0, 0), pipeline_mode=once)
    whole = [
        pl.BlockSpec(r.shape, lambda n, me: (0, 0), pipeline_mode=once) for r in (*bundles, *weights)
    ]
    out = jax.ShapeDtypeStruct((CHIPS, k, s), jnp.float32)
    vmem = 2 * p * (total + CORES * s) + 4 * CHIPS * k * s * (2 + len(before)) + 4 * total * TILE
    return pl.pallas_call(
        functools.partial(multiply_kernel, names, len(bundles), k, steps, not before),
        out_shape=[out, out],
        grid_spec=pltpu.PrefetchScalarGridSpec(
            num_scalar_prefetch=1,
            grid=(2 * steps,),
            in_specs=whole + [kept] * len(before),
            out_specs=[kept, kept],
            scratch_shapes=[pltpu.VMEM((total, TILE), jnp.float32)],
        ),
        compiler_params=pltpu.CompilerParams(vmem_limit_bytes=vmem + (1 << 20)),
        cost_estimate=pl.CostEstimate(
            flops=4 * total * p * s, bytes_accessed=2 * p * (total + 2 * s) + 16 * CHIPS * k * s, transcendentals=0
        ),
        name=name,
    )(me, *bundles, *weights, *before)


def across_floors(rows, at):
    width = rows.shape[1] // len(at)

    def parts(*owners):
        return jnp.concatenate(
            [lax.dynamic_slice_in_dim(rows, q * width, width, 1) for q in owners], axis=1
        )

    def swap(value, by):
        return lax.ppermute(value, "floor", [(f, f ^ by) for f in range(len(at))])

    two = parts(at[0], at[3]) + swap(parts(at[1], at[2]), 1)
    return two[:, :width] + swap(two[:, width:], 3)


def local(samples, operator):
    me = lax.axis_index("tm")
    core = me % CORES
    half = samples.shape[2] // CORES
    own = operator[0]

    def columns(rows, which):
        return lax.dynamic_slice_in_dim(rows, which * half, half, 1)

    mine, theirs = lax.optimization_barrier(
        (columns(samples[0], core), columns(samples[0], 1 - core))
    )
    theirs = lax.ppermute(theirs, "tm", OTHER_CORE)
    block = jnp.concatenate(
        [jnp.where(core == 0, mine, theirs), jnp.where(core == 0, theirs, mine)], axis=0
    )
    at = me.reshape(1)

    def names(bundles):
        return [d for n, _ in bundles for d in n]

    def rows(bundles):
        return [r for _, r in bundles]

    chain = {}
    held = [((OWN,), block)]
    held = held + send(held, PHASES[0], chain)
    other = columns(after(own, block), 1 - core)
    mine = columns(after(own, *rows(held)), core)
    sent = []
    held = held + send(held, PHASES[1], chain, (), sent)
    other = lax.ppermute(after(other, *sent), "tm", OTHER_CORE)
    chain[ZZ] = [other]
    weights = (mine, other)
    got = send(held, PHASES[2], chain, (other,))
    early = multiply(at, names(held), rows(held), weights, (), "early")
    mid_blocks = got
    got = send(held + mid_blocks, PHASES[3], chain, early[:1])
    shared = send_shared(held + mid_blocks, chain, early[0])
    mid = multiply(at, names(mid_blocks), rows(mid_blocks), weights, early, "mid")
    last = send_last(got, chain, mid[0])
    keep, out = multiply(
        at,
        names(got) + [SHARING[0][1], SHARED, SHARING[1][1], LAST],
        rows(got) + shared + last,
        weights,
        mid,
        "late",
    )

    both = keep + lax.ppermute(out, "tm", OTHER_CORE)
    floor = lax.axis_index("floor")
    floors = [floor ^ n for n in range(lax.axis_size("floor"))]
    sums = lax.all_to_all(both, "tm", 0, 0, tiled=True, axis_index_groups=SAME_CORE).sum(0)
    return across_floors(sums, floors)[None].astype(jnp.bfloat16)


def solution(mesh):
    placed = (P("tm", None, "floor"), P("tm", None, "floor"))
    return jax.shard_map(
        local, mesh=mesh, in_specs=placed, out_specs=P("tm", None, "floor"), check_vma=False
    )
```

```python
import functools

import jax
import jax.numpy as jnp
from jax import lax
from jax.experimental import pallas as pl
from jax.experimental.pallas import tpu as pltpu
from jax.sharding import PartitionSpec as P

Y, Z, X, CORES = 4, 2, 4, 2
CHIPS = Y * Z * X

XP, XM, YP, YM, ZZ = (1, 0, 0), (3, 0, 0), (0, 1, 0), (0, 3, 0), (0, 0, 1)
LINKS = (XP, XM, YP, YM, ZZ)
OWN, LAST = (0, 0, 0), (2, 2, 1)
FINISH = (XM, YM)
PHASES = (
    ((XM, ((3, 0, 0),)), (YP, ((0, 1, 0),)), (ZZ, ((0, 0, 1),)), (XP, ((1, 0, 0),)), (YM, ((0, 3, 0),))),
    (
        (YP, ((0, 2, 0), (3, 1, 0))),
        (XM, ((2, 0, 0), (3, 0, 1))),
        (XP, ((1, 0, 1), (1, 1, 0))),
        (YM, ((1, 3, 0), (3, 3, 0))),
    ),
    (
        (XM, ((3, 2, 0), (2, 1, 0))),
        (YM, ((2, 3, 0), (3, 3, 1))),
        (YP, ((1, 1, 1), (3, 1, 1))),
        (ZZ, ((0, 2, 1), (1, 3, 1))),
        (XP, ((2, 0, 1), (1, 2, 0))),
    ),
    ((ZZ, ((0, 1, 1), (0, 3, 1))), (YM, ((3, 2, 1),)), (XM, ((2, 3, 1),))),
)
SHARED = (2, 2, 0)
SHARING = ((XP, (2, 1, 1)), (YP, (1, 2, 1)))


def number(y, z, x, core):
    return ((y * Z + z) * X + x) * CORES + core


def moved(d, link):
    return ((d[0] - link[0]) % X, (d[1] - link[1]) % Y, (d[2] - link[2]) % Z)


def pairs(link):
    return [
        (number(y, z, x, c), number((y + link[1]) % Y, (z + link[2]) % Z, (x + link[0]) % X, c))
        for y in range(Y)
        for z in range(Z)
        for x in range(X)
        for c in range(CORES)
    ]


OTHER_CORE = [(2 * i + c, 2 * i + 1 - c) for i in range(CHIPS) for c in range(CORES)]
SAME_CORE = [[2 * i + c for i in range(CHIPS)] for c in range(CORES)]


def fetch(held, wanted):
    for names, rows in held:
        if names == wanted:
            return rows
    k = held[0][1].shape[0] // len(held[0][0])
    parts = []
    for name in wanted:
        names, rows = next((n, r) for n, r in held if name in n)
        at = names.index(name) * k
        parts.append(rows if len(names) == 1 else rows[at : at + k])
    return parts[0] if len(parts) == 1 else jnp.concatenate(parts, axis=0)


def after(value, *others):
    return lax.optimization_barrier((value, *others))[0]


def send(held, phase, chain, waits=(), sent=None):
    rows = [fetch(held, tuple(moved(d, link) for d in names)) for link, names in phase]
    got = []
    for (link, names), r in zip(phase, rows):
        ties = chain.get(link, []) + list(waits)
        if ties:
            r = after(r, *ties)
        if sent is not None:
            sent.append(r)
        chain[link] = [lax.ppermute(r, "tm", pairs(link))]
        got.append((names, chain[link][0]))
    return got


def send_last(held, chain, wait):
    rows = [fetch(held, (moved(LAST, link),)) for link in FINISH]
    k = rows[0].shape[0] // len(FINISH)
    return [
        lax.ppermute(after(r[n * k : (n + 1) * k], wait, *chain[link]), "tm", pairs(link))
        for n, (link, r) in enumerate(zip(FINISH, rows))
    ]


def send_shared(held, chain, wait):
    (first, before), (second, behind) = SHARING
    k = held[0][1].shape[0] // len(held[0][0])
    parts = (
        (first, [fetch(held, (moved(before, first),)), fetch(held, (moved(SHARED, first),))[: k // 2]]),
        (second, [fetch(held, (moved(SHARED, second),))[k // 2 :], fetch(held, (moved(behind, second),))]),
    )
    got = []
    for link, rows in parts:
        rows = after(jnp.concatenate(rows, axis=0), wait, *chain[link])
        chain[link] = [lax.ppermute(rows, "tm", pairs(link))]
        got.append(chain[link][0])
    return got


def source(me, d):
    chip = me // CORES
    x, z, y = chip % X, (chip // X) % Z, chip // (X * Z)
    return (((y - d[1] + Y) % Y) * Z + (z - d[2] + Z) % Z) * X + (x - d[0] + X) % X


def multiply_kernel(names, count, k, steps, first, *refs):
    me_ref, refs = refs[0], refs[1:]
    bundles, refs = refs[:count], refs[count:]
    weights, refs = refs[:CORES], refs[CORES:]
    keep, out, rows = refs[-3:]
    n = pl.program_id(0)
    me = me_ref[0]
    core, chip = me % CORES, me // CORES
    width = weights[0].shape[0] // steps

    @pl.when(n == 0)
    def _():
        if first:
            keep[...] = jnp.zeros_like(keep)
            out[...] = jnp.zeros_like(out)
        else:
            keep[...] = refs[0][...]
            out[...] = refs[1][...]

    def place(even, odd, shift, columns):
        for b, d in enumerate(names):
            to = source(me, d) + chip
            after = to + shift

            @pl.when(to < CHIPS)
            def _():
                even[to, :, columns] += rows[2 * b * k : (2 * b + 1) * k]

            @pl.when(after < CHIPS)
            def _():
                odd[after, :, columns] += rows[(2 * b + 1) * k : (2 * b + 2) * k]

    for which, tiles in enumerate(weights):
        for step in range(steps):

            @pl.when(n == which * steps + step)
            def _():
                left = jnp.concatenate([b[...] for b in bundles], axis=0)
                rows[...] = lax.dot_general(
                    left,
                    tiles[step * width : (step + 1) * width],
                    (((1,), (1,)), ((), ())),
                    preferred_element_type=jnp.float32,
                )

    for step in range(steps):
        columns = slice(step * width, (step + 1) * width)

        @pl.when(n == step)
        def _():
            place(keep, out, core, columns)

        @pl.when(n == steps + step)
        def _():
            place(out, keep, 1 - core, columns)


TILE = 512


def multiply(me, names, bundles, weights, before, name):
    total, p = sum(r.shape[0] for r in bundles), bundles[0].shape[1]
    s = weights[0].shape[0]
    k, steps = total // (2 * len(names)), s // TILE
    once = pl.Buffered(1)
    kept = pl.BlockSpec((CHIPS, k, s), lambda n, me: (0, 0, 0), pipeline_mode=once)
    whole = [
        pl.BlockSpec(r.shape, lambda n, me: (0, 0), pipeline_mode=once) for r in (*bundles, *weights)
    ]
    out = jax.ShapeDtypeStruct((CHIPS, k, s), jnp.float32)
    vmem = 2 * p * (total + CORES * s) + 4 * CHIPS * k * s * (2 + len(before)) + 4 * total * TILE
    return pl.pallas_call(
        functools.partial(multiply_kernel, names, len(bundles), k, steps, not before),
        out_shape=[out, out],
        grid_spec=pltpu.PrefetchScalarGridSpec(
            num_scalar_prefetch=1,
            grid=(2 * steps,),
            in_specs=whole + [kept] * len(before),
            out_specs=[kept, kept],
            scratch_shapes=[pltpu.VMEM((total, TILE), jnp.float32)],
        ),
        compiler_params=pltpu.CompilerParams(vmem_limit_bytes=vmem + (1 << 20)),
        cost_estimate=pl.CostEstimate(
            flops=4 * total * p * s, bytes_accessed=2 * p * (total + 2 * s) + 16 * CHIPS * k * s, transcendentals=0
        ),
        name=name,
    )(me, *bundles, *weights, *before)


def across_floors(rows, at):
    width = rows.shape[1] // len(at)

    def parts(*owners):
        return jnp.concatenate(
            [lax.dynamic_slice_in_dim(rows, q * width, width, 1) for q in owners], axis=1
        )

    def swap(value, by):
        return lax.ppermute(value, "floor", [(f, f ^ by) for f in range(len(at))])

    two = parts(at[0], at[3]) + swap(parts(at[1], at[2]), 1)
    return two[:, :width] + swap(two[:, width:], 3)


def local(samples, operator):
    me = lax.axis_index("tm")
    core = me % CORES
    half = samples.shape[2] // CORES
    own = operator[0]

    def columns(rows, which):
        return lax.dynamic_slice_in_dim(rows, which * half, half, 1)

    mine, theirs = lax.optimization_barrier(
        (columns(samples[0], core), columns(samples[0], 1 - core))
    )
    theirs = lax.ppermute(theirs, "tm", OTHER_CORE)
    block = jnp.concatenate(
        [jnp.where(core == 0, mine, theirs), jnp.where(core == 0, theirs, mine)], axis=0
    )
    at = me.reshape(1)

    def names(bundles):
        return [d for n, _ in bundles for d in n]

    def rows(bundles):
        return [r for _, r in bundles]

    chain = {}
    held = [((OWN,), block)]
    held = held + send(held, PHASES[0], chain)
    other = columns(after(own, block), 1 - core)
    mine = columns(after(own, *rows(held)), core)
    sent = []
    held = held + send(held, PHASES[1], chain, (), sent)
    other = lax.ppermute(after(other, *sent), "tm", OTHER_CORE)
    chain[ZZ] = [other]
    weights = (mine, other)
    got = send(held, PHASES[2], chain, (other,))
    early = multiply(at, names(held), rows(held), weights, (), "early")
    mid_blocks = got
    got = send(held + mid_blocks, PHASES[3], chain, early[:1])
    shared = send_shared(held + mid_blocks, chain, early[0])
    mid = multiply(at, names(mid_blocks), rows(mid_blocks), weights, early, "mid")
    last = send_last(got, chain, mid[0])
    keep, out = multiply(
        at,
        names(got) + [SHARING[0][1], SHARED, SHARING[1][1], LAST],
        rows(got) + shared + last,
        weights,
        mid,
        "late",
    )

    both = keep + lax.ppermute(out, "tm", OTHER_CORE)
    floor = lax.axis_index("floor")
    floors = [floor ^ n for n in range(lax.axis_size("floor"))]
    sums = lax.all_to_all(both, "tm", 0, 0, tiled=True, axis_index_groups=SAME_CORE).sum(0)
    return across_floors(sums, floors)[None].astype(jnp.bfloat16)


def solution(mesh):
    placed = (P("tm", None, "floor"), P("tm", None, "floor"))
    return jax.shard_map(
        local, mesh=mesh, in_specs=placed, out_specs=P("tm", None, "floor"), check_vma=False
    )
```

```python
import functools

import jax
import jax.numpy as jnp
from jax import lax
from jax.experimental import pallas as pl
from jax.experimental.pallas import tpu as pltpu
from jax.sharding import PartitionSpec as P

Y, Z, X, CORES = 4, 2, 4, 2
CHIPS = Y * Z * X

XP, XM, YP, YM, ZZ = (1, 0, 0), (3, 0, 0), (0, 1, 0), (0, 3, 0), (0, 0, 1)
LINKS = (XP, XM, YP, YM, ZZ)
OWN, LAST = (0, 0, 0), (2, 2, 1)
FINISH = (XM, YM)
PHASES = (
    ((XM, ((3, 0, 0),)), (YP, ((0, 1, 0),)), (ZZ, ((0, 0, 1),)), (XP, ((1, 0, 0),)), (YM, ((0, 3, 0),))),
    (
        (YP, ((0, 2, 0), (3, 1, 0))),
        (XM, ((2, 0, 0), (3, 0, 1))),
        (XP, ((1, 0, 1), (1, 1, 0))),
        (YM, ((1, 3, 0), (3, 3, 0))),
    ),
    (
        (XM, ((3, 2, 0), (2, 1, 0))),
        (YM, ((2, 3, 0), (3, 3, 1))),
        (YP, ((1, 1, 1), (3, 1, 1))),
        (ZZ, ((0, 2, 1), (1, 3, 1))),
        (XP, ((2, 0, 1), (1, 2, 0))),
    ),
    ((ZZ, ((0, 1, 1), (0, 3, 1))), (YM, ((3, 2, 1),)), (XM, ((2, 3, 1),))),
)
SHARED = (2, 2, 0)
SHARING = ((XP, (2, 1, 1)), (YP, (1, 2, 1)))


def number(y, z, x, core):
    return ((y * Z + z) * X + x) * CORES + core


def moved(d, link):
    return ((d[0] - link[0]) % X, (d[1] - link[1]) % Y, (d[2] - link[2]) % Z)


def pairs(link):
    return [
        (number(y, z, x, c), number((y + link[1]) % Y, (z + link[2]) % Z, (x + link[0]) % X, c))
        for y in range(Y)
        for z in range(Z)
        for x in range(X)
        for c in range(CORES)
    ]


OTHER_CORE = [(2 * i + c, 2 * i + 1 - c) for i in range(CHIPS) for c in range(CORES)]
SAME_CORE = [[2 * i + c for i in range(CHIPS)] for c in range(CORES)]


def fetch(held, wanted):
    for names, rows in held:
        if names == wanted:
            return rows
    k = held[0][1].shape[0] // len(held[0][0])
    parts = []
    for name in wanted:
        names, rows = next((n, r) for n, r in held if name in n)
        at = names.index(name) * k
        parts.append(rows if len(names) == 1 else rows[at : at + k])
    return parts[0] if len(parts) == 1 else jnp.concatenate(parts, axis=0)


def after(value, *others):
    return lax.optimization_barrier((value, *others))[0]


def send(held, phase, chain, waits=(), sent=None):
    rows = [fetch(held, tuple(moved(d, link) for d in names)) for link, names in phase]
    got = []
    for (link, names), r in zip(phase, rows):
        ties = chain.get(link, []) + list(waits)
        if ties:
            r = after(r, *ties)
        if sent is not None:
            sent.append(r)
        chain[link] = [lax.ppermute(r, "tm", pairs(link))]
        got.append((names, chain[link][0]))
    return got


def send_last(held, wait):
    rows = [fetch(held, (moved(LAST, link),)) for link in FINISH]
    k = rows[0].shape[0] // len(FINISH)
    return [
        lax.ppermute(after(r[n * k : (n + 1) * k], wait), "tm", pairs(link))
        for n, (link, r) in enumerate(zip(FINISH, rows))
    ]


def send_shared(held, chain, wait):
    (first, before), (second, behind) = SHARING
    k = held[0][1].shape[0] // len(held[0][0])
    parts = (
        (first, [fetch(held, (moved(before, first),)), fetch(held, (moved(SHARED, first),))[: k // 2]]),
        (second, [fetch(held, (moved(SHARED, second),))[k // 2 :], fetch(held, (moved(behind, second),))]),
    )
    got = []
    for link, rows in parts:
        rows = after(jnp.concatenate(rows, axis=0), wait, *chain[link])
        chain[link] = [lax.ppermute(rows, "tm", pairs(link))]
        got.append(chain[link][0])
    return got


def source(me, d):
    chip = me // CORES
    x, z, y = chip % X, (chip // X) % Z, chip // (X * Z)
    return (((y - d[1] + Y) % Y) * Z + (z - d[2] + Z) % Z) * X + (x - d[0] + X) % X


def multiply_kernel(names, count, k, steps, first, *refs):
    me_ref, refs = refs[0], refs[1:]
    bundles, refs = refs[:count], refs[count:]
    weights, refs = refs[:CORES], refs[CORES:]
    keep, out, rows = refs[-3:]
    n = pl.program_id(0)
    me = me_ref[0]
    core, chip = me % CORES, me // CORES
    width = weights[0].shape[0] // steps

    @pl.when(n == 0)
    def _():
        if first:
            keep[...] = jnp.zeros_like(keep)
            out[...] = jnp.zeros_like(out)
        else:
            keep[...] = refs[0][...]
            out[...] = refs[1][...]

    def place(even, odd, shift, columns):
        for b, d in enumerate(names):
            to = source(me, d) + chip
            after = to + shift

            @pl.when(to < CHIPS)
            def _():
                even[to, :, columns] += rows[2 * b * k : (2 * b + 1) * k]

            @pl.when(after < CHIPS)
            def _():
                odd[after, :, columns] += rows[(2 * b + 1) * k : (2 * b + 2) * k]

    for which, tiles in enumerate(weights):
        for step in range(steps):

            @pl.when(n == which * steps + step)
            def _():
                left = jnp.concatenate([b[...] for b in bundles], axis=0)
                rows[...] = lax.dot_general(
                    left,
                    tiles[step * width : (step + 1) * width],
                    (((1,), (1,)), ((), ())),
                    preferred_element_type=jnp.float32,
                )

    for step in range(steps):
        columns = slice(step * width, (step + 1) * width)

        @pl.when(n == step)
        def _():
            place(keep, out, core, columns)

        @pl.when(n == steps + step)
        def _():
            place(out, keep, 1 - core, columns)


TILE = 512


def multiply(me, names, bundles, weights, before, name):
    total, p = sum(r.shape[0] for r in bundles), bundles[0].shape[1]
    s = weights[0].shape[0]
    k, steps = total // (2 * len(names)), s // TILE
    once = pl.Buffered(1)
    kept = pl.BlockSpec((CHIPS, k, s), lambda n, me: (0, 0, 0), pipeline_mode=once)
    whole = [
        pl.BlockSpec(r.shape, lambda n, me: (0, 0), pipeline_mode=once) for r in (*bundles, *weights)
    ]
    out = jax.ShapeDtypeStruct((CHIPS, k, s), jnp.float32)
    vmem = 2 * p * (total + CORES * s) + 4 * CHIPS * k * s * (2 + len(before)) + 4 * total * TILE
    return pl.pallas_call(
        functools.partial(multiply_kernel, names, len(bundles), k, steps, not before),
        out_shape=[out, out],
        grid_spec=pltpu.PrefetchScalarGridSpec(
            num_scalar_prefetch=1,
            grid=(2 * steps,),
            in_specs=whole + [kept] * len(before),
            out_specs=[kept, kept],
            scratch_shapes=[pltpu.VMEM((total, TILE), jnp.float32)],
        ),
        compiler_params=pltpu.CompilerParams(vmem_limit_bytes=vmem + (1 << 20)),
        cost_estimate=pl.CostEstimate(
            flops=4 * total * p * s, bytes_accessed=2 * p * (total + 2 * s) + 16 * CHIPS * k * s, transcendentals=0
        ),
        name=name,
    )(me, *bundles, *weights, *before)


def across_floors(rows, at):
    width = rows.shape[1] // len(at)

    def parts(*owners):
        return jnp.concatenate(
            [lax.dynamic_slice_in_dim(rows, q * width, width, 1) for q in owners], axis=1
        )

    def swap(value, by):
        return lax.ppermute(value, "floor", [(f, f ^ by) for f in range(len(at))])

    two = parts(at[0], at[3]) + swap(parts(at[1], at[2]), 1)
    return two[:, :width] + swap(two[:, width:], 3)


def local(samples, operator):
    me = lax.axis_index("tm")
    core = me % CORES
    half = samples.shape[2] // CORES
    own = operator[0]

    def columns(rows, which):
        return lax.dynamic_slice_in_dim(rows, which * half, half, 1)

    mine, theirs = lax.optimization_barrier(
        (columns(samples[0], core), columns(samples[0], 1 - core))
    )
    theirs = lax.ppermute(theirs, "tm", OTHER_CORE)
    block = jnp.concatenate(
        [jnp.where(core == 0, mine, theirs), jnp.where(core == 0, theirs, mine)], axis=0
    )
    at = me.reshape(1)

    def names(bundles):
        return [d for n, _ in bundles for d in n]

    def rows(bundles):
        return [r for _, r in bundles]

    chain = {}
    held = [((OWN,), block)]
    held = held + send(held, PHASES[0], chain)
    other = columns(after(own, block), 1 - core)
    mine = columns(after(own, *rows(held)), core)
    sent = []
    held = held + send(held, PHASES[1], chain, (), sent)
    other = lax.ppermute(after(other, *sent), "tm", OTHER_CORE)
    chain[ZZ] = [other]
    weights = (mine, other)
    got = send(held, PHASES[2], chain, (other,))
    early = multiply(at, names(held), rows(held), weights, (), "early")
    mid_blocks = got
    got = send(held + mid_blocks, PHASES[3], chain, early[:1])
    shared = send_shared(held + mid_blocks, chain, early[0])
    mid = multiply(at, names(mid_blocks), rows(mid_blocks), weights, early, "mid")
    last = send_last(got, mid[0])
    keep, out = multiply(
        at,
        names(got) + [SHARING[0][1], SHARED, SHARING[1][1], LAST],
        rows(got) + shared + last,
        weights,
        mid,
        "late",
    )

    both = keep + lax.ppermute(out, "tm", OTHER_CORE)
    floor = lax.axis_index("floor")
    floors = [floor ^ n for n in range(lax.axis_size("floor"))]
    sums = lax.all_to_all(both, "tm", 0, 0, tiled=True, axis_index_groups=SAME_CORE).sum(0)
    return across_floors(sums, floors)[None].astype(jnp.bfloat16)


def solution(mesh):
    placed = (P("tm", None, "floor"), P("tm", None, "floor"))
    return jax.shard_map(
        local, mesh=mesh, in_specs=placed, out_specs=P("tm", None, "floor"), check_vma=False
    )
```
